32 devices in a mesh: row: 8 (over y, x, core), col: 4 (over z).
Axes of the slice: x: 2, y: 2, z: 4, core: 2. Of those that a mesh axis runs over, the one named last changes fastest.
Arguments:
- right_sides: float32 [64, 32768], P(None, ('row', 'col'))
- diag_tiles: float32 [32, 1024, 1024], P(('row', 'col')), as said below
- low_rank: float32 [32, 4, 8, 2, 12, 1024], P('row', 'col'), as said below
- tile_ranks: int32 [32, 4, 8], P('row', 'col'), may hold values from 1 to 12, as said below
- inv_factor: float32 [256, 8, 128, 128], P(('row', 'col')), as said below
- sub_sizes: int32 [64], replicated, may hold values from 1 to 8, 256 in all
Outputs:
- solution: float32 [64, 32768], P(None, ('row', 'col'))
- residual: float32 [64, 32768], P(None, ('row', 'col'))
The draws below stay inside these ranges and needn't reach their ends.
Inputs may be any that keep to these rules, and one draw needn't show every extreme that they name: `low_rank`: tile (j, i) holds the two factors of tile (i, j) in swapped order, and a diagonal tile's two factors are equal, so S is symmetric. `tile_ranks`: the rank of tile (i, j) equals that of tile (j, i); diagonal tiles have rank 12. `diag_tiles`: each tile is symmetric positive definite. `inv_factor`: the block at distance 0 of every span is lower triangular with a positive diagonal. `sub_sizes`: the sizes sum to 256.
All inputs are finite; a program needn't handle non-finite values.
Results may differ from the reference program's by a relative error of at most 0.0003.
Values sent between devices are 32-bit elements; how exact they have to be, the bound alone decides.
A program may use at most 128 MiB of HBM per device.

```python
import math
import jax
import jax.numpy as jnp
import numpy as np
from jax import lax

RHS = 64
TILE = 1024
RANK = 12
SPAN = 128
MAXC = 8
STRIDE = 4
GROUPS = 8
NT = 32
ORDER = 32768
NCHUNK = 256
SUBS = 64


def draw_right_sides(key, part):
    fraction = lax.iota(jnp.float32, ORDER) / ORDER
    rising = 1.0 + 2.0 * fraction
    values = jax.random.normal(key, (RHS, ORDER), jnp.float32) * rising
    return values


def draw_diag_tiles(key, part):
    noise_key, diag_key = jax.random.split(key)
    noises = jax.random.normal(noise_key, (NT, TILE, TILE), jnp.float32)
    symmetric = (noises + jnp.swapaxes(noises, 1, 2)) * (0.42 / math.sqrt(TILE))
    diagonal = jnp.exp(jax.random.uniform(diag_key, (NT, TILE, 1), jnp.float32, math.log(2.2), math.log(4.4)))
    identity = (lax.iota(jnp.int32, TILE)[:, None] == lax.iota(jnp.int32, TILE)[None, :]).astype(jnp.float32)
    return symmetric + diagonal * identity[None]


def draw_low_rank(key, part):
    spread_scale = 0.45 * (ORDER * RANK) ** (-0.25)
    slot_ids = lax.iota(jnp.int32, STRIDE)
    group_ids = lax.iota(jnp.int32, GROUPS)

    def one_tile(row_index, col_slot, group):
        col_index = group * STRIDE + col_slot
        pair_index = jnp.minimum(row_index, col_index) * NT + jnp.maximum(row_index, col_index)
        tile_key = jax.random.fold_in(key, pair_index)
        noises = jax.random.normal(tile_key, (2, RANK, TILE), jnp.float32)
        left_part = jnp.where(row_index < col_index, noises[1], noises[0])
        right_part = jnp.where(row_index > col_index, noises[1], noises[0])
        return jnp.stack([left_part, right_part]) * spread_scale

    def tile_row(row_index):

        def by_slot(col_slot):

            def by_group(group):
                return one_tile(row_index, col_slot, group)
            return jax.vmap(by_group)(group_ids)
        return jax.vmap(by_slot)(slot_ids)
    return lax.map(tile_row, lax.iota(jnp.int32, NT))


def draw_tile_ranks(key, part):
    drawn = jax.random.randint(key, (NT, NT), 1, RANK + 1)
    row_ids = lax.iota(jnp.int32, NT)[:, None]
    col_ids = lax.iota(jnp.int32, NT)[None, :]
    mirrored = jnp.where(row_ids > col_ids, drawn, drawn.T)
    mirrored = jnp.where(row_ids == col_ids, RANK, mirrored)
    return mirrored.reshape(NT, GROUPS, STRIDE).transpose(0, 2, 1)


def draw_inv_factor(key, part):
    noise_key, diag_key = jax.random.split(key)
    shape_all = (NCHUNK, MAXC, SPAN, SPAN)
    noises = jax.random.normal(noise_key, shape_all, jnp.float32)
    out_ids = lax.iota(jnp.int32, SPAN)[:, None]
    in_ids = lax.iota(jnp.int32, SPAN)[None, :]
    strict = (in_ids < out_ids).astype(jnp.float32)
    identity = (in_ids == out_ids).astype(jnp.float32)
    pivots = jnp.exp(jax.random.uniform(diag_key, (NCHUNK, 1, SPAN, 1), jnp.float32, 0.0, math.log(2.0)))
    slot_zero = noises * strict * (0.4 / math.sqrt(SPAN)) + pivots * identity
    others = noises * (0.4 / math.sqrt(SPAN * MAXC))
    first_slot = (lax.iota(jnp.int32, MAXC) == 0)[None, :, None, None]
    return jnp.where(first_slot, slot_zero, others)


def length_profile(count, total, bound, lean):
    portions = [(1 << 20) // math.isqrt(grade ** lean) + 1 for grade in range(2, count + 1)]
    surplus, given = total - bound - (count - 1), [1] * (count - 1)
    while surplus > 0:
        free = [i for i in range(count - 1) if given[i] < bound]
        mass, remaining = sum([portions[i] for i in free]), surplus
        for i in free:
            addition = min(bound - given[i], max(1, remaining * portions[i] // mass), surplus)
            given[i] = given[i] + addition
            surplus = surplus - addition
    return np.array([bound] + given)


def ragged(key, number_of, total, most, lean):
    if number_of == 2:
        one = jax.random.randint(key, (), max(1, total - most), min(most, total - 1) + 1)
        return jnp.stack([one, total - one])
    lengths = jnp.asarray(length_profile(number_of, total, most, lean), jnp.int32)
    pairs = (number_of - 1) // 2
    giver, receiver = lengths[1:1 + 2 * pairs:2], lengths[2:2 + 2 * pairs:2]
    slack = jnp.minimum(giver - 1, most - receiver)
    moved = jax.random.randint(jax.random.fold_in(key, 1), (pairs,), 0, 1 << 20) % (slack + 1)
    lengths = lengths.at[1:1 + 2 * pairs:2].set(giver - moved).at[2:2 + 2 * pairs:2].set(receiver + moved)
    return lengths[jax.random.permutation(jax.random.fold_in(key, 2), number_of)]


def setup_inputs(seed: int = 0) -> dict:
    key_list = jax.random.split(jax.random.key(seed), 7)
    return {
        "right_sides": draw_right_sides(jax.random.fold_in(key_list[6], 71), 0),
        "diag_tiles": draw_diag_tiles(jax.random.fold_in(key_list[6], 71), 0),
        "low_rank": draw_low_rank(jax.random.fold_in(key_list[6], 71), 0),
        "tile_ranks": draw_tile_ranks(jax.random.fold_in(key_list[6], 71), 0),
        "inv_factor": draw_inv_factor(jax.random.fold_in(key_list[6], 71), 0),
        "sub_sizes": ragged(key_list[5], SUBS, NCHUNK, MAXC, 2).astype(jnp.int32),
    }


finest = lax.Precision.HIGHEST

def span_weights(span_ids, sub_sizes):
    ending = jnp.cumsum(sub_sizes).astype(jnp.int32)
    opening = (ending - sub_sizes).astype(jnp.int32)
    inside = (span_ids[:, None] >= opening[None, :]) & (span_ids[:, None] < ending[None, :])
    position = span_ids - jnp.sum(jnp.where(inside, opening[None, :], 0), axis=1).astype(jnp.int32)
    return (lax.iota(jnp.int32, MAXC)[None, :] <= position[:, None]).astype(jnp.float32)

def precondition(vector, inv_factor, weights):
    blocks = vector.reshape(RHS, NCHUNK, SPAN)
    padded = jnp.pad(blocks, ((0, 0), (MAXC, 0), (0, 0)))
    windows = jnp.stack([padded[:, MAXC - behind:MAXC - behind + NCHUNK] for behind in range(MAXC)], axis=2)
    windows = windows * weights[None, :, :, None]
    forward = jnp.einsum('ltji,klti->klj', inv_factor, windows, precision=finest)
    spread = jnp.einsum('ltji,klj->klti', inv_factor, forward, precision=finest) * weights[None, :, :, None]
    result = jnp.zeros_like(blocks)
    for behind in range(MAXC):
        result = result + jnp.pad(spread[:, behind:, behind], ((0, 0), (0, behind), (0, 0)))
    return result.reshape(RHS, ORDER)

def operate(vector, diag_tiles, low_rank, tile_ranks):
    tiles_in = vector.reshape(RHS, NT, TILE)
    local_part = jnp.einsum('kit,its->kis', tiles_in, diag_tiles, precision=finest)

    def tile_row(row_item):
        factors, row_ranks = row_item
        ordered = jnp.swapaxes(factors, 0, 1).reshape(NT, 2, RANK, TILE)
        ordered_ranks = jnp.swapaxes(row_ranks, 0, 1).reshape(NT)
        weight = (lax.iota(jnp.int32, RANK)[None, :] < ordered_ranks[:, None]).astype(jnp.float32)
        coeffs = jnp.einsum('jqt,kjt->jqk', ordered[:, 1], tiles_in, precision=finest) * weight[:, :, None]
        return jnp.einsum('jqt,jqk->kt', ordered[:, 0], coeffs, precision=finest)
    far_part = lax.map(tile_row, (low_rank, tile_ranks))
    return (local_part + jnp.swapaxes(far_part, 0, 1)).reshape(RHS, ORDER)

def solve_spd(matrix, target):
    factor = jnp.linalg.cholesky(matrix)
    return jax.scipy.linalg.cho_solve((factor, True), target)

def gram_of(first_block, second_block):
    return jnp.dot(first_block, second_block.T, precision=finest)

def apply_coeffs(coeffs, block_rows):
    return jnp.dot(coeffs.T, block_rows, precision=finest)

def reference(right_sides, diag_tiles, low_rank, tile_ranks, inv_factor, sub_sizes):
    weights = span_weights(lax.iota(jnp.int32, NCHUNK), sub_sizes)
    residual = right_sides
    search = precondition(residual, inv_factor, weights)
    rho_now = gram_of(search, residual)
    images = operate(search, diag_tiles, low_rank, tile_ranks)
    step_size = solve_spd(gram_of(search, images), rho_now)
    solution = apply_coeffs(step_size, search)
    residual = residual - apply_coeffs(step_size, images)
    precond = precondition(residual, inv_factor, weights)
    rho_next = gram_of(precond, residual)
    beta_mix = solve_spd(rho_now, rho_next)
    search = precond + apply_coeffs(beta_mix, search)
    images = operate(search, diag_tiles, low_rank, tile_ranks)
    step_size = solve_spd(gram_of(search, images), rho_next)
    solution = solution + apply_coeffs(step_size, search)
    residual = residual - apply_coeffs(step_size, images)
    return (solution, residual)
```

```python
import functools
import math

import jax
import jax.numpy as jnp
from jax import lax
from jax.experimental import pallas as pl
from jax.experimental.pallas import tpu as pltpu
from jax.sharding import PartitionSpec as P

MESH = pl.DeviceIdType.MESH
F32 = jnp.float32
BF16 = jnp.bfloat16
LOW = 8
LANES = 128


def split(x):
    high = x.astype(BF16)
    return high, (x - high.astype(F32)).astype(BF16)


def stacked(x):
    high, low = split(x)
    return jnp.concatenate([high, low], axis=0)


def dot_nt(a, b):
    return lax.dot_general(a, b, (((1,), (1,)), ((), ())), preferred_element_type=F32)


def dot_nn(a, b):
    return lax.dot_general(a, b, (((1,), (0,)), ((), ())), preferred_element_type=F32)


def product3(dot, both, high, low):
    rows = both.shape[0] // 2
    first = dot(both, high)
    return first[:rows] + (first[rows:] + dot(both[:rows], low))


def gram(a, b):
    return lax.dot_general(
        a, b, (((1,), (1,)), ((), ())), precision=lax.Precision.HIGHEST, preferred_element_type=F32
    )


def mixed(coeffs, rows):
    return jnp.dot(coeffs, rows, precision=lax.Precision.HIGHEST, preferred_element_type=F32)


def eliminate(work):
    count, width = work.shape
    block = 4
    row_ids = lax.broadcasted_iota(jnp.int32, work.shape, 0)
    for k in range(0, count, block):
        columns = [jnp.broadcast_to(work[:, k + j : k + j + 1], work.shape) for j in range(block)]
        rows = [work[k + i : k + i + 1, :] for i in range(block)]
        heads = [[columns[j][k + i : k + i + 1, :] for j in range(block)] for i in range(block)]
        for i in range(block):
            inverse = 1.0 / heads[i][i]
            rows[i] = rows[i] * inverse
            for j in range(i + 1, block):
                heads[i][j] = heads[i][j] * inverse
            for other in range(block):
                if other != i:
                    factor = heads[other][i]
                    rows[other] = rows[other] - factor * rows[i]
                    for j in range(i + 1, block):
                        heads[other][j] = heads[other][j] - factor * heads[i][j]
        update = columns[0] * rows[0]
        for j in range(1, block):
            update = update + columns[j] * rows[j]
        work = work - update
        for i in range(block):
            work = jnp.where(row_ids == k + i, rows[i], work)
    return work


def solved(work):
    return eliminate(work).T[work.shape[0] :, :]


def kernel(
    rows, cols, pieces, rank,
    x_hbm, diag_ref, factor_ref, ranks_ref, inv_ref, sizes_ref,
    sol_ref, res_ref,
    x_ref, inv_f32, inv_cat, diag_f32, diag_hi, diag_lo, u_f32, u_hi, u_lo,
    factor_f32, packed, joined, halo_in, back_in, spread, fwd, doubled, vec_z, vec_p, vec_q, vec_n, pair,
    acc_wide, acc_low, coef_out, coef_in, sum_row, sum_col, nothing, sizes_vmem, ranks,
    inv_sem, diag_sem, factor_sem, small_sem, own_sem, u_send, u_recv, halo_send, halo_recv, back_send, back_recv,
    coef_send, coef_recv, row_send, row_recv, col_send, col_recv,
):
    my_row, my_col = lax.axis_index("row"), lax.axis_index("col")
    total = rows * cols
    me = my_row * cols + my_col
    rhs, tile = x_hbm.shape
    spans, reach, span, _ = inv_ref.shape
    halo = (reach - 1) * span
    wide = reach * span
    offset = tile - halo
    half = rank // 2

    def coords(device):
        return (device // cols, device % cols)

    following = coords((me + 1) % total)
    previous = coords((me + total - 1) % total)

    coef_in[...] = jnp.zeros_like(coef_in)
    back_in[...] = jnp.zeros_like(back_in)
    nothing[...] = jnp.zeros_like(nothing)

    barrier = pltpu.get_barrier_semaphore()

    def greet(step, carry):
        peer_row = (my_row + step) % rows
        for turn in range(cols):
            pl.semaphore_signal(
                barrier, inc=1, device_id=(peer_row, (my_col + turn) % cols), device_id_type=MESH
            )
        return carry

    for turn in range(1, cols):
        pl.semaphore_signal(
            barrier, inc=1, device_id=(my_row, (my_col + turn) % cols), device_id_type=MESH
        )
    lax.fori_loop(1, rows, greet, 0)

    factor_copy = pltpu.make_async_copy(factor_ref, factor_f32, factor_sem)
    factor_copy.start()
    ranks_copy = pltpu.make_async_copy(ranks_ref, ranks, small_sem.at[0])
    ranks_copy.start()
    sizes_copy = pltpu.make_async_copy(sizes_ref, sizes_vmem, small_sem.at[1])
    sizes_copy.start()
    x_copy = pltpu.make_async_copy(x_hbm, x_ref, small_sem.at[2])
    x_copy.start()
    for a in range(spans):
        for t in range(reach):
            copy = pltpu.make_async_copy(
                inv_ref.at[a, t],
                inv_f32.at[a, :, (reach - 1 - t) * span : (reach - t) * span],
                inv_sem.at[a],
            )
            copy.start()
    diag_copy = pltpu.make_async_copy(diag_ref.at[0], diag_f32, diag_sem)
    diag_copy.start()
    groups = rows
    tail = rank - LOW
    step_rows = 2 * (tile // LANES)

    def at_rows(ref, index, size):
        return ref.at[pl.ds(pl.multiple_of(index * size, size), size), :]

    def take(base, side, first, size, limit):
        ids = first + lax.broadcasted_iota(jnp.int32, (size, LANES), 0)
        parts = [
            factor_f32[pl.ds(base + first * step_rows + 2 * i + side, size, stride=step_rows), :]
            for i in range(tile // LANES)
        ]
        return jnp.concatenate([jnp.where(ids < limit, part, 0.0) for part in parts], axis=1)

    ranks_copy.wait()
    factor_copy.wait()

    def block(base, side, limit):
        rest = take(base, side, LOW, tail, limit)
        rest = jnp.concatenate([rest[:, : tile // 2], rest[:, tile // 2 :]], axis=0)
        return take(base, side, 0, LOW, limit), rest

    def pack(k, carry):
        for a in range(cols):
            base = (a * groups + k) * rank * step_rows
            first, rest = block(base, 1, ranks[a, 0, k])
            packed[k, a * LOW : (a + 1) * LOW, :tile] = first
            packed[k, a * LOW : (a + 1) * LOW, tile:] = rest
        base = (my_col * groups + k) * rank * step_rows
        where = pl.ds(pl.multiple_of((k * cols + my_col) * LOW, LOW), LOW)
        first, rest = block(base, 0, ranks[my_col, 0, k])
        u_f32[where, :tile] = first
        u_f32[where, tile:] = rest
        return carry

    lax.fori_loop(0, groups, pack, 0)

    for turn in range(1, cols):
        a = (my_col + turn) % cols
        pltpu.make_async_copy(
            at_rows(packed.at[my_row], a, LOW), at_rows(u_f32, my_row * cols + a, LOW), own_sem.at[1]
        ).start()
    pl.semaphore_wait(barrier, total - 1)

    def remote(src, dst, send, recv, device):
        return pltpu.make_async_remote_copy(
            src_ref=src, dst_ref=dst, send_sem=send, recv_sem=recv, device_id=device,
            device_id_type=MESH,
        )

    def halo_copy(src, call, c):
        lo, hi = pieces[c]
        return remote(
            src.at[:, offset + lo : offset + hi], halo_in.at[call, :, lo:hi],
            halo_send.at[call, c], halo_recv.at[call, c], following,
        )

    def back_copy(call, c):
        lo, hi = pieces[c]
        return remote(
            spread.at[call, :, lo:hi], back_in.at[call, :, offset + lo : offset + hi],
            back_send.at[call, c], back_recv.at[call, c], previous,
        )

    def send_halo(src, call, which):
        @pl.when(me != total - 1)
        def _():
            for c in which:
                halo_copy(src, call, c).start()

        @pl.when(me == 0)
        def _():
            for c in which:
                lo, hi = pieces[c]
                pltpu.make_async_copy(
                    nothing.at[:, lo:hi], halo_in.at[call, :, lo:hi], halo_recv.at[call, c]
                ).start()

    def send_back(call):
        @pl.when(me != 0)
        def _():
            for c in range(len(pieces)):
                back_copy(call, c).start()

        @pl.when(me == total - 1)
        def _():
            for c, (lo, hi) in enumerate(pieces):
                pltpu.make_async_copy(
                    nothing.at[:, lo:hi], back_in.at[call, :, offset + lo : offset + hi],
                    back_recv.at[call, c],
                ).start()

    send_halo(x_hbm, 0, range(len(pieces)))

    def send_factors(step, carry):
        peer = (my_row + step) % rows
        for turn in range(1, cols):
            a = (my_col + turn) % cols
            remote(at_rows(packed.at[peer], a, LOW), at_rows(u_f32, my_row * cols + a, LOW),
                   u_send, u_recv, (peer, my_col)).start()
        return carry

    lax.fori_loop(1, rows, send_factors, 0)
    x_copy.wait()
    sizes_copy.wait()

    subs = sizes_ref.shape[1]
    sizes = jnp.broadcast_to(sizes_vmem[...].astype(F32), (subs, subs))
    down = lax.broadcasted_iota(jnp.int32, (subs, subs), 0)
    across = lax.broadcasted_iota(jnp.int32, (subs, subs), 1)
    opening = jnp.sum(jnp.where(across < down, sizes, 0.0), axis=1, keepdims=True)
    behind = (reach - 1) - lax.broadcasted_iota(jnp.int32, (1, wide), 1) // span
    behind = behind.astype(F32)

    joined[:, halo:] = stacked(x_ref[...])

    for a in range(spans):
        for t in range(reach):
            pltpu.make_async_copy(
                inv_ref.at[a, t], inv_f32.at[a, :, t * span : (t + 1) * span], inv_sem.at[a]
            ).wait()
        number = (me * spans + a).astype(F32)
        start = jnp.max(jnp.where(opening <= number, opening, 0.0), axis=0, keepdims=True)
        mask = jnp.where(behind <= number - start, 1.0, 0.0)
        high, low = split(inv_f32[a] * mask)
        inv_cat[a, :span] = high
        inv_cat[a, span:] = low

    def quarters(product):
        first = product[:rhs, :span]
        return first + (product[rhs:, :span] + (product[:rhs, span:] + product[rhs:, span:]))

    def halves(product):
        return product[:rhs] + product[rhs:]

    def forward_own():
        for a in range(spans):
            skip = max(0, halo - a * span)
            fwd[a] = quarters(
                dot_nt(joined[:, a * span + skip : a * span + wide], inv_cat[a, :, skip:])
            )

    def finish(a):
        both = stacked(fwd[a])
        doubled[a] = jnp.concatenate([both, both], axis=1)

    def boundary(call):
        for a in range(spans):
            if a * span >= halo:
                finish(a)
        for c, (lo, hi) in enumerate(pieces):
            halo_copy(x_ref, call, c).wait_recv()
            joined[:, lo:hi] = stacked(halo_in[call, :, lo:hi])
            for a in range(spans):
                first = max(lo, a * span)
                if first < hi:
                    fwd[a] += quarters(dot_nt(
                        joined[:, first:hi], inv_cat[a, :, first - a * span : hi - a * span]
                    ))
            for a in range(spans):
                if lo <= a * span < hi:
                    finish(a)
                    spread[call, :, a * span : halo] += halves(
                        dot_nn(doubled[a], inv_cat[a, :, : halo - a * span])
                    )
        send_back(call)

    def backward_own(call):
        for a in range(spans):
            skip = max(0, halo - a * span)
            spread[call, :, a * span + skip : a * span + wide] += halves(
                dot_nn(doubled[a], inv_cat[a, :, skip:])
            )

    def returned(call, c):
        lo, hi = pieces[c]
        back_copy(call, c).wait_recv()
        first = offset + lo if lo else 0
        last = offset + hi
        return first, last, spread[call, :, halo + first : halo + last] + back_in[call, :, first:last]

    def add_coeffs(c, first, last, piece):
        both = stacked(piece)
        pair[:, first:last] = both
        wide_part = dot_nt(u_hi[:, first:last], both)
        low_part = dot_nt(u_lo[:, first:last], both[:rhs])
        if c:
            acc_wide[...] += wide_part
            acc_low[...] += low_part
        else:
            acc_wide[...] = wide_part
            acc_low[...] = low_part

    def send_coeffs(call):
        coeffs = acc_wide[:, :rhs] + (acc_wide[:, rhs:] + acc_low[...])
        middle = total * LOW
        coef_out[call, :, :, :rhs] = coeffs[:middle].reshape(total, LOW, rhs)
        coef_out[call, :, :, rhs:] = coeffs[middle:].reshape(total, LOW, rhs)

        def send(peer_row, peer_col):
            remote(coef_out.at[call, peer_row * cols + peer_col, :half, :],
                   coef_in.at[call, me, :half, :],
                   coef_send.at[call], coef_recv.at[call], (peer_row, peer_col)).start()

        low_side = 1 - my_col // (cols // 2)

        def send_row(step, carry):
            peer_row = (my_row + step) % rows
            for n in range(cols - 1):
                far = low_side * (cols - 1 - n) + (1 - low_side) * n
                beyond = (far - my_col + cols - 1) // cols
                before = (my_col - far + cols - 1) // cols
                far = far - low_side * (1 - beyond) + (1 - low_side) * (1 - before)
                send(peer_row, far)
            return carry

        lax.fori_loop(0, rows, send_row, 0)
        for step in range(1, rows):
            send((my_row + step) % rows, my_col)
        pltpu.make_async_copy(
            coef_out.at[call, me], coef_in.at[call, me], own_sem.at[2 + call]
        ).start()

    def flat(ref, call):
        return ref[call].reshape(total * LOW, 2 * rhs).T

    def wait_coeffs(call):
        every = coef_out.at[call, : total - 1, :half, :]
        pltpu.make_async_copy(every, every, coef_recv.at[call]).wait()
        pltpu.make_async_copy(
            coef_out.at[call, me], coef_in.at[call, me], own_sem.at[2 + call]
        ).wait()
        return flat(coef_in, call)

    def far_gram(mine, others):
        product = gram(mine, others)
        return product[:rhs, :rhs] + product[rhs:, rhs:]

    height = rhs // 2

    def start_sum(value, call):
        sum_row[call, my_row] = jnp.concatenate([value[:height], value[height:]], axis=1)
        for step in range(1, rows):
            mine = sum_row.at[call, my_row]
            remote(mine, mine, row_send.at[call],
                   row_recv.at[call], ((my_row + step) % rows, my_col)).start()

    def middle_sum(call):
        piece = sum_row.at[call, : rows - 1]
        pltpu.make_async_copy(piece, piece, row_recv.at[call]).wait()
        sum_col[call, my_col] = jnp.sum(sum_row[call], axis=0)
        for step in range(1, cols):
            mine = sum_col.at[call, my_col]
            remote(mine, mine, col_send.at[call],
                   col_recv.at[call], (my_row, (my_col + step) % cols)).start()

    def end_sum(call):
        piece = sum_col.at[call, : cols - 1]
        pltpu.make_async_copy(piece, piece, col_recv.at[call]).wait()
        halves_ = jnp.sum(sum_col[call], axis=0)
        return jnp.concatenate([halves_[:, :rhs], halves_[:, rhs:]], axis=0)

    spread[...] = jnp.zeros_like(spread)
    forward_own()
    boundary(0)
    backward_own(0)
    diag_copy.wait()

    def split_diag(step, carry):
        where = pl.ds(pl.multiple_of(step * span, span), span)
        high, low = split(diag_f32[where, :])
        diag_hi[where, :] = high
        diag_lo[where, :] = low
        return carry

    lax.fori_loop(0, tile // span, split_diag, 0)
    own_piece = u_f32.at[: (cols - 1) * LOW, :]
    pltpu.make_async_copy(own_piece, own_piece, own_sem.at[1]).wait()
    others = u_f32.at[: (rows - 1) * (cols - 1) * LOW, :]
    pltpu.make_async_copy(others, others, u_recv).wait()
    level = lax.broadcasted_iota(jnp.int32, (2 * LOW, tile), 0) % LOW
    empty = jnp.zeros((LOW - tail, tile), F32)

    def split_factors(step, carry):
        where = pl.ds(pl.multiple_of(step * 2 * LOW, 2 * LOW), 2 * LOW)
        first = u_f32[where, :tile]
        high, low = split(jnp.where(level < half, first, 0.0))
        u_hi[where, :] = high
        u_lo[where, :] = low
        rest = u_f32[where, tile:]
        parts = []
        for top in (0, LOW):
            parts.append(jnp.concatenate(
                [rest[top : top + tail], rest[top + tail : top + 2 * tail]], axis=1
            ))
            parts.append(empty)
        moved = pltpu.roll(first, 2 * LOW - (half - tail), 0)
        second = jnp.concatenate(parts, axis=0)
        second = jnp.where((level >= tail) & (level < half), moved, second)
        high, low = split(second)
        later = pl.ds(pl.multiple_of(total * LOW + step * 2 * LOW, 2 * LOW), 2 * LOW)
        u_hi[later, :] = high
        u_lo[later, :] = low
        return carry

    lax.fori_loop(0, total // 2, split_factors, 0)
    for c in range(len(pieces)):
        first, last, piece = returned(0, c)
        vec_z[:, first:last] = piece
        add_coeffs(c, first, last, piece)
    send_coeffs(0)
    start_sum(gram(vec_z[...], x_ref[...]), 3)
    near = product3(dot_nn, pair[...], diag_hi[...], diag_lo[...])
    vec_n[...] = near
    own0 = gram(vec_z[...], near)
    mine = flat(coef_out, 0)
    middle_sum(3)
    turned = wait_coeffs(0)

    def far_pieces(turned):
        both = stacked(jnp.concatenate([turned[:rhs], turned[rhs:]], axis=1))
        for c, (lo, hi) in enumerate(pieces):
            first = offset + lo if lo else 0
            last = offset + hi
            yield c, first, last, product3(
                dot_nn, both, u_hi[:, first:last], u_lo[:, first:last]
            )

    for c, first, last, piece in far_pieces(turned):
        vec_q[:, first:last] = vec_n[:, first:last] + piece
        send_halo(vec_q, 1, (c,))
    start_sum(own0 + far_gram(mine, turned), 0)
    joined[:, halo:] = stacked(vec_q[...])
    forward_own()
    rho0 = end_sum(3)
    square = (rhs, rhs)
    identity = (
        lax.broadcasted_iota(jnp.int32, square, 0) == lax.broadcasted_iota(jnp.int32, square, 1)
    ).astype(F32)
    inverse = eliminate(jnp.concatenate([rho0, identity], axis=1))[:, rhs:]
    middle_sum(0)
    boundary(1)
    backward_own(1)
    curve = end_sum(0)
    alpha0 = solved(jnp.concatenate([curve, rho0], axis=1))
    res_ref[...] = x_ref[...] - mixed(alpha0, vec_q[...])
    for c in range(len(pieces)):
        first, last, piece = returned(1, c)
        piece = vec_z[:, first:last] - mixed(alpha0, piece)
        vec_p[:, first:last] = piece
        add_coeffs(c, first, last, piece)
    send_coeffs(1)
    start_sum(gram(vec_p[...], res_ref[...]), 1)
    near = product3(dot_nn, pair[...], diag_hi[...], diag_lo[...])
    vec_n[...] = near
    own1 = gram(vec_p[...], near)
    mine = flat(coef_out, 1)
    sol_ref[...] = mixed(alpha0, vec_z[...])
    middle_sum(1)
    turned = wait_coeffs(1)
    start_sum(own1 + far_gram(mine, turned), 2)
    for c, first, last, piece in far_pieces(turned):
        vec_n[:, first:last] += piece
    middle_sum(2)
    rho1 = end_sum(1)
    beta0_t = mixed(inverse, rho1).T
    known = gram(mixed(beta0_t, curve), beta0_t)
    vec_p[...] += mixed(beta0_t, vec_z[...])
    vec_n[...] += mixed(beta0_t, vec_q[...])
    own = end_sum(2)
    alpha1 = solved(jnp.concatenate([own - known, rho1], axis=1))
    sol_ref[...] += mixed(alpha1, vec_p[...])
    res_ref[...] -= mixed(alpha1, vec_n[...])

    pltpu.make_async_copy(others, others, u_send).wait()

    @pl.when(me != total - 1)
    def _():
        for call in range(2):
            for c in range(len(pieces)):
                halo_copy(x_ref, call, c).wait_send()

    @pl.when(me != 0)
    def _():
        for call in range(2):
            for c in range(len(pieces)):
                back_copy(call, c).wait_send()

    for call in range(2):
        every = coef_out.at[call, : total - 1, :half, :]
        pltpu.make_async_copy(every, every, coef_send.at[call]).wait()
    for call in range(4):
        piece = sum_row.at[call, : rows - 1]
        pltpu.make_async_copy(piece, piece, row_send.at[call]).wait()
        piece = sum_col.at[call, : cols - 1]
        pltpu.make_async_copy(piece, piece, col_send.at[call]).wait()


def write_out(sol_ref, res_ref, sol_out, res_out, sems):
    copies = [
        pltpu.make_async_copy(sol_ref, sol_out, sems.at[0]),
        pltpu.make_async_copy(res_ref, res_out, sems.at[1]),
    ]
    for copy in copies:
        copy.start()
    for copy in copies:
        copy.wait()


def body(rows, cols, right_sides, diag_tiles, low_rank, tile_ranks, inv_factor, sub_sizes):
    rhs, tile = right_sides.shape
    spans, reach, span, _ = inv_factor.shape
    tile_rows, _, groups, _, rank, _ = low_rank.shape
    total = rows * cols
    halo = (reach - 1) * span
    lanes = tile // LANES
    factor = low_rank.reshape(tile_rows, groups, 2, rank, lanes, LANES)
    factor = factor.transpose(0, 1, 3, 4, 2, 5).reshape(-1, LANES)
    pieces, high = [], halo
    while high > 0:
        pieces.append((max(0, high - 2 * span), high))
        high = pieces[-1][0]
    count = len(pieces)
    in_hbm = pl.BlockSpec(memory_space=pltpu.HBM)
    vmem = pl.BlockSpec(memory_space=pltpu.VMEM)
    dma = pltpu.SemaphoreType.DMA
    out = jax.ShapeDtypeStruct((rhs, tile), F32)
    sizes = sub_sizes.reshape(1, -1)
    buffers = [
        pltpu.VMEM((rhs, tile), F32),
        pltpu.VMEM((spans, span, reach * span), F32),
        pltpu.VMEM((spans, 2 * span, reach * span), BF16),
        pltpu.VMEM((tile, tile), F32),
        pltpu.VMEM((tile, tile), BF16),
        pltpu.VMEM((tile, tile), BF16),
        pltpu.VMEM((total * LOW, tile + tile // 2), F32),
        pltpu.VMEM((2 * total * LOW, tile), BF16),
        pltpu.VMEM((2 * total * LOW, tile), BF16),
        pltpu.VMEM(factor.shape, F32),
        pltpu.VMEM((groups, tile_rows * LOW, tile + tile // 2), F32),
        pltpu.VMEM((2 * rhs, halo + tile), BF16),
        pltpu.VMEM((2, rhs, halo), F32),
        pltpu.VMEM((2, rhs, tile), F32),
        pltpu.VMEM((2, rhs, halo + tile), F32),
        pltpu.VMEM((spans, rhs, span), F32),
        pltpu.VMEM((spans, 2 * rhs, 2 * span), BF16),
        pltpu.VMEM((rhs, tile), F32),
        pltpu.VMEM((rhs, tile), F32),
        pltpu.VMEM((rhs, tile), F32),
        pltpu.VMEM((rhs, tile), F32),
        pltpu.VMEM((2 * rhs, tile), BF16),
        pltpu.VMEM((2 * total * LOW, 2 * rhs), F32),
        pltpu.VMEM((2 * total * LOW, rhs), F32),
        pltpu.VMEM((2, total, LOW, 2 * rhs), F32),
        pltpu.VMEM((2, total, LOW, 2 * rhs), F32),
        pltpu.VMEM((4, rows, rhs // 2, 2 * rhs), F32),
        pltpu.VMEM((4, cols, rhs // 2, 2 * rhs), F32),
        pltpu.VMEM((rhs, halo), F32),
        pltpu.VMEM(sizes.shape, jnp.int32),
    ]
    held = sum(math.prod(b.shape) * jnp.dtype(b.dtype).itemsize for b in buffers)
    grant = min(held + (8 << 20), 62 << 20)
    operands = [
        pltpu.with_memory_space_constraint(array, pltpu.HBM)
        for array in (right_sides, diag_tiles, factor, tile_ranks, inv_factor, sizes)
    ]
    results = pl.pallas_call(
        functools.partial(kernel, rows, cols, tuple(pieces), rank),
        out_shape=(pltpu.VMEM((rhs, tile), F32), pltpu.VMEM((rhs, tile), F32)),
        in_specs=[in_hbm] * 6,
        out_specs=(vmem, vmem),
        scratch_shapes=buffers + [
            pltpu.SMEM(tile_ranks.shape, jnp.int32),
            dma((spans,)), dma, dma, dma((3,)), dma((4,)), dma, dma,
            dma((2, count)), dma((2, count)), dma((2, count)), dma((2, count)),
            dma((2,)), dma((2,)), dma((4,)), dma((4,)), dma((4,)), dma((4,)),
        ],
        compiler_params=pltpu.CompilerParams(
            collective_id=0, has_side_effects=True, vmem_limit_bytes=grant
        ),
    )(*operands)
    return pl.pallas_call(
        write_out,
        out_shape=(out, out),
        in_specs=[vmem, vmem],
        out_specs=(in_hbm, in_hbm),
        scratch_shapes=[dma((2,))],
        compiler_params=pltpu.CompilerParams(vmem_limit_bytes=1 << 20),
    )(*[pltpu.with_memory_space_constraint(result, pltpu.VMEM) for result in results])


def solution(mesh):
    rows, cols = mesh.shape["row"], mesh.shape["col"]
    placed = (
        P(None, ("row", "col")),
        P(("row", "col"), None, None),
        P("row", "col", None, None, None, None),
        P("row", "col", None),
        P(("row", "col"), None, None, None),
        P(),
    )
    return jax.shard_map(
        functools.partial(body, rows, cols),
        mesh=mesh,
        in_specs=placed,
        out_specs=(P(None, ("row", "col")), P(None, ("row", "col"))),
        check_vma=False,
    )
```

```python
import functools
import math

import jax
import jax.numpy as jnp
from jax import lax
from jax.experimental import pallas as pl
from jax.experimental.pallas import tpu as pltpu
from jax.sharding import PartitionSpec as P

MESH = pl.DeviceIdType.MESH
F32 = jnp.float32
BF16 = jnp.bfloat16
LOW = 8
LANES = 128


def split(x):
    high = x.astype(BF16)
    return high, (x - high.astype(F32)).astype(BF16)


def stacked(x):
    high, low = split(x)
    return jnp.concatenate([high, low], axis=0)


def dot_nt(a, b):
    return lax.dot_general(a, b, (((1,), (1,)), ((), ())), preferred_element_type=F32)


def dot_nn(a, b):
    return lax.dot_general(a, b, (((1,), (0,)), ((), ())), preferred_element_type=F32)


def product3(dot, both, high, low):
    rows = both.shape[0] // 2
    first = dot(both, high)
    return first[:rows] + (first[rows:] + dot(both[:rows], low))


def gram(a, b):
    return lax.dot_general(
        a, b, (((1,), (1,)), ((), ())), precision=lax.Precision.HIGHEST, preferred_element_type=F32
    )


def mixed(coeffs, rows):
    return jnp.dot(coeffs, rows, precision=lax.Precision.HIGHEST, preferred_element_type=F32)


def eliminate(work):
    count, width = work.shape
    block = 8
    row_ids = lax.broadcasted_iota(jnp.int32, work.shape, 0)
    for k in range(0, count, block):
        columns = [jnp.broadcast_to(work[:, k + j : k + j + 1], work.shape) for j in range(block)]
        rows = [work[k + i : k + i + 1, :] for i in range(block)]
        heads = [[columns[j][k + i : k + i + 1, :] for j in range(block)] for i in range(block)]
        for i in range(block):
            inverse = 1.0 / heads[i][i]
            rows[i] = rows[i] * inverse
            for j in range(i + 1, block):
                heads[i][j] = heads[i][j] * inverse
            for other in range(block):
                if other != i:
                    factor = heads[other][i]
                    rows[other] = rows[other] - factor * rows[i]
                    for j in range(i + 1, block):
                        heads[other][j] = heads[other][j] - factor * heads[i][j]
        terms = [columns[j] * rows[j] for j in range(block)]
        while len(terms) > 1:
            terms = [terms[j] + terms[j + 1] for j in range(0, len(terms), 2)]
        work = work - terms[0]
        for i in range(block):
            work = jnp.where(row_ids == k + i, rows[i], work)
    return work


def solved(work):
    return eliminate(work).T[work.shape[0] :, :]


def kernel(
    rows, cols, pieces, rank,
    x_hbm, diag_ref, factor_ref, ranks_ref, inv_ref, sizes_ref,
    sol_ref, res_ref,
    x_ref, inv_f32, inv_cat, diag_f32, diag_hi, diag_lo, u_f32, u_hi, u_lo,
    factor_f32, packed, joined, halo_in, back_in, spread, fwd, doubled, vec_z, vec_p, vec_q, vec_n, pair,
    acc_wide, acc_low, coef_out, coef_in, sum_row, sum_col, nothing, sizes_vmem, ranks,
    inv_sem, diag_sem, factor_sem, small_sem, own_sem, u_send, u_recv, halo_send, halo_recv, back_send, back_recv,
    coef_send, coef_recv, row_send, row_recv, col_send, col_recv, known,
):
    my_row, my_col = lax.axis_index("row"), lax.axis_index("col")
    total = rows * cols
    me = my_row * cols + my_col
    rhs, tile = x_hbm.shape
    spans, reach, span, _ = inv_ref.shape
    halo = (reach - 1) * span
    wide = reach * span
    offset = tile - halo
    half = rank // 2

    def coords(device):
        return (device // cols, device % cols)

    following = coords((me + 1) % total)
    previous = coords((me + total - 1) % total)

    coef_in[...] = jnp.zeros_like(coef_in)
    back_in[...] = jnp.zeros_like(back_in)
    nothing[...] = jnp.zeros_like(nothing)

    barrier = pltpu.get_barrier_semaphore()

    def greet(semaphore, device):
        pl.semaphore_signal(semaphore, inc=1, device_id=device, device_id_type=MESH)

    for turn in range(1, cols):
        greet(barrier, (my_row, (my_col + turn) % cols))
    for step in range(1, rows):
        greet(barrier, ((my_row + step) % rows, my_col))

    @pl.when((my_col == cols - 1) & (me != total - 1))
    def _():
        greet(barrier, following)

    @pl.when((my_col == 0) & (me != 0))
    def _():
        greet(barrier, previous)

    factor_copy = pltpu.make_async_copy(factor_ref, factor_f32, factor_sem)
    factor_copy.start()
    ranks_copy = pltpu.make_async_copy(ranks_ref, ranks, small_sem.at[0])
    ranks_copy.start()
    sizes_copy = pltpu.make_async_copy(sizes_ref, sizes_vmem, small_sem.at[1])
    sizes_copy.start()
    x_copy = pltpu.make_async_copy(x_hbm, x_ref, small_sem.at[2])
    x_copy.start()
    groups = rows
    tail = rank - LOW
    step_rows = 2 * (tile // LANES)

    def at_rows(ref, index, size):
        return ref.at[pl.ds(pl.multiple_of(index * size, size), size), :]

    def take(base, side, first, size, limit):
        ids = first + lax.broadcasted_iota(jnp.int32, (size, LANES), 0)
        parts = [
            factor_f32[pl.ds(base + first * step_rows + 2 * i + side, size, stride=step_rows), :]
            for i in range(tile // LANES)
        ]
        return jnp.concatenate([jnp.where(ids < limit, part, 0.0) for part in parts], axis=1)

    ranks_copy.wait()
    factor_copy.wait()
    for a in range(spans):
        for t in range(reach):
            copy = pltpu.make_async_copy(
                inv_ref.at[a, t],
                inv_f32.at[a, :, (reach - 1 - t) * span : (reach - t) * span],
                inv_sem.at[a],
            )
            copy.start()
    diag_copy = pltpu.make_async_copy(diag_ref.at[0], diag_f32, diag_sem)
    diag_copy.start()

    def block(base, side, limit):
        rest = take(base, side, LOW, tail, limit)
        rest = jnp.concatenate([rest[:, : tile // 2], rest[:, tile // 2 :]], axis=0)
        return take(base, side, 0, LOW, limit), rest

    def differ(difference, most):
        square = difference * difference
        return (square + most * most - 1) // (most * most)

    def by_column(k, a):
        if rows % 4:
            return 0
        opposite = 1 - differ(k // 2 + my_row // 2 - (rows // 2 - 1), rows)
        near = 1 - differ((a - my_col) * (a - my_col) - 1, cols * cols)
        return opposite * near

    def pack(k, carry):
        for a in range(cols):
            base = (a * groups + k) * rank * step_rows
            first, rest = block(base, 1 - by_column(k, a), ranks[a, 0, k])
            packed[k, a * LOW : (a + 1) * LOW, :tile] = first
            packed[k, a * LOW : (a + 1) * LOW, tile:] = rest
        base = (my_col * groups + k) * rank * step_rows
        where = pl.ds(pl.multiple_of((k * cols + my_col) * LOW, LOW), LOW)
        first, rest = block(base, 0, ranks[my_col, 0, k])
        u_f32[where, :tile] = first
        u_f32[where, tile:] = rest
        return carry

    lax.fori_loop(0, groups, pack, 0)

    for turn in range(1, cols):
        a = (my_col + turn) % cols
        pltpu.make_async_copy(
            at_rows(packed.at[my_row], a, LOW), at_rows(u_f32, my_row * cols + a, LOW), own_sem.at[1]
        ).start()
    wraps = (1 - differ(my_col - (cols - 1), cols)) * differ(me - (total - 1), total)
    wrapped = (1 - differ(my_col, cols)) * differ(me, total)
    pl.semaphore_wait(barrier, rows + cols - 2 + wraps + wrapped)

    def remote(src, dst, send, recv, device):
        return pltpu.make_async_remote_copy(
            src_ref=src, dst_ref=dst, send_sem=send, recv_sem=recv, device_id=device,
            device_id_type=MESH,
        )

    def halo_copy(src, call, c):
        lo, hi = pieces[c]
        return remote(
            src.at[:, offset + lo : offset + hi], halo_in.at[call, :, lo:hi],
            halo_send.at[call, c], halo_recv.at[call, c], following,
        )

    def back_copy(call, c):
        lo, hi = pieces[c]
        return remote(
            spread.at[call, :, lo:hi], back_in.at[call, :, offset + lo : offset + hi],
            back_send.at[call, c], back_recv.at[call, c], previous,
        )

    def send_halo(src, call, which):
        @pl.when(me != total - 1)
        def _():
            for c in which:
                halo_copy(src, call, c).start()

        fill_first(call, which)

    def fill_first(call, which):

        @pl.when(me == 0)
        def _():
            for c in which:
                lo, hi = pieces[c]
                pltpu.make_async_copy(
                    nothing.at[:, lo:hi], halo_in.at[call, :, lo:hi], halo_recv.at[call, c]
                ).start()

    def send_back(call):
        @pl.when(me != 0)
        def _():
            for c in range(len(pieces)):
                back_copy(call, c).start()

        @pl.when(me == total - 1)
        def _():
            for c, (lo, hi) in enumerate(pieces):
                pltpu.make_async_copy(
                    nothing.at[:, lo:hi], back_in.at[call, :, offset + lo : offset + hi],
                    back_recv.at[call, c],
                ).start()

    every_piece = range(len(pieces))

    send_halo(x_hbm, 0, every_piece)

    def send_factors(step, carry):
        peer = (my_row + step) % rows
        for turn in range(1, cols):
            a = (my_col + turn) % cols
            column = by_column(peer, a)
            slot = (1 - column) * (my_row * cols + a) + column * (peer * cols + my_col)
            place = (peer + column * (my_row - peer), my_col + column * (a - my_col))
            remote(at_rows(packed.at[peer], a, LOW), at_rows(u_f32, slot, LOW),
                   u_send, u_recv, place).start()
        return carry

    lax.fori_loop(1, rows, send_factors, 0)
    for step in range(1, rows):
        greet(known, ((my_row + step) % rows, my_col))
    x_copy.wait()
    sizes_copy.wait()

    subs = sizes_ref.shape[1]
    sizes = jnp.broadcast_to(sizes_vmem[...].astype(F32), (subs, subs))
    down = lax.broadcasted_iota(jnp.int32, (subs, subs), 0)
    across = lax.broadcasted_iota(jnp.int32, (subs, subs), 1)
    opening = jnp.sum(jnp.where(across < down, sizes, 0.0), axis=1, keepdims=True)
    behind = (reach - 1) - lax.broadcasted_iota(jnp.int32, (1, wide), 1) // span
    behind = behind.astype(F32)

    joined[:, halo:] = stacked(x_ref[...])

    for a in range(spans):
        for t in range(reach):
            pltpu.make_async_copy(
                inv_ref.at[a, t], inv_f32.at[a, :, t * span : (t + 1) * span], inv_sem.at[a]
            ).wait()
        number = (me * spans + a).astype(F32)
        start = jnp.max(jnp.where(opening <= number, opening, 0.0), axis=0, keepdims=True)
        mask = jnp.where(behind <= number - start, 1.0, 0.0)
        high, low = split(inv_f32[a] * mask)
        inv_cat[a, :span] = high
        inv_cat[a, span:] = low


    def quarters(product):
        first = product[:rhs, :span]
        return first + (product[rhs:, :span] + (product[:rhs, span:] + product[rhs:, span:]))

    def halves(product):
        return product[:rhs] + product[rhs:]

    def forward_own():
        for a in range(spans):
            skip = max(0, halo - a * span)
            fwd[a] = quarters(
                dot_nt(joined[:, a * span + skip : a * span + wide], inv_cat[a, :, skip:])
            )

    def finish(a):
        both = stacked(fwd[a])
        doubled[a] = jnp.concatenate([both, both], axis=1)

    def boundary(call):
        for a in range(spans):
            if a * span >= halo:
                finish(a)
        for c, (lo, hi) in enumerate(pieces):
            halo_copy(x_ref, call, c).wait_recv()
            joined[:, lo:hi] = stacked(halo_in[call, :, lo:hi])
            for a in range(spans):
                first = max(lo, a * span)
                if first < hi:
                    fwd[a] += quarters(dot_nt(
                        joined[:, first:hi], inv_cat[a, :, first - a * span : hi - a * span]
                    ))
            for a in range(spans):
                if lo <= a * span < hi:
                    finish(a)
                    spread[call, :, a * span : halo] += halves(
                        dot_nn(doubled[a], inv_cat[a, :, : halo - a * span])
                    )
        send_back(call)

    def backward_own(call):
        for a in range(spans):
            skip = max(0, halo - a * span)
            spread[call, :, a * span + skip : a * span + wide] += halves(
                dot_nn(doubled[a], inv_cat[a, :, skip:])
            )

    def returned(call, c):
        lo, hi = pieces[c]
        back_copy(call, c).wait_recv()
        first = offset + lo if lo else 0
        last = offset + hi
        return first, last, spread[call, :, halo + first : halo + last] + back_in[call, :, first:last]

    def add_coeffs(c, first, last, piece):
        both = stacked(piece)
        pair[:, first:last] = both
        wide_part = dot_nt(u_hi[:, first:last], both)
        low_part = dot_nt(u_lo[:, first:last], both[:rhs])
        if c:
            acc_wide[...] += wide_part
            acc_low[...] += low_part
        else:
            acc_wide[...] = wide_part
            acc_low[...] = low_part

    def send_coeffs(call):
        coeffs = acc_wide[:, :rhs] + (acc_wide[:, rhs:] + acc_low[...])
        middle = total * LOW
        coef_out[call, :, :, :rhs] = coeffs[:middle].reshape(total, LOW, rhs)
        coef_out[call, :, :, rhs:] = coeffs[middle:].reshape(total, LOW, rhs)

        def send(peer_row, peer_col):
            remote(coef_out.at[call, peer_row * cols + peer_col, :half, :],
                   coef_in.at[call, me, :half, :],
                   coef_send.at[call], coef_recv.at[call], (peer_row, peer_col)).start()

        low_side = 1 - my_col // (cols // 2)

        def send_row(step, carry):
            peer_row = (my_row + step) % rows
            for n in range(cols - 1):
                far = low_side * (cols - 1 - n) + (1 - low_side) * n
                beyond = (far - my_col + cols - 1) // cols
                before = (my_col - far + cols - 1) // cols
                far = far - low_side * (1 - beyond) + (1 - low_side) * (1 - before)
                send(peer_row, far)
            return carry

        lax.fori_loop(0, rows, send_row, 0)
        for step in range(1, rows):
            send((my_row + step) % rows, my_col)
        pltpu.make_async_copy(
            coef_out.at[call, me], coef_in.at[call, me], own_sem.at[2 + call]
        ).start()

    def flat(ref, call):
        return stacked(ref[call].reshape(total * LOW, 2 * rhs).T)

    def wait_coeffs(call):
        every = coef_out.at[call, : total - 1, :half, :]
        pltpu.make_async_copy(every, every, coef_recv.at[call]).wait()
        pltpu.make_async_copy(
            coef_out.at[call, me], coef_in.at[call, me], own_sem.at[2 + call]
        ).wait()
        return flat(coef_in, call)

    def far_gram(mine, others):
        product = dot_nt(mine, others)
        width = 2 * rhs
        square = product[:width, :width] + (
            product[width:, :width] + (product[:width, width:] + product[width:, width:])
        )
        return square[:rhs, :rhs] + square[rhs:, rhs:]

    height = rhs // 2

    def start_sum(value, call):
        sum_row[call, my_row] = jnp.concatenate([value[:height], value[height:]], axis=1)
        for step in range(1, rows):
            mine = sum_row.at[call, my_row]
            remote(mine, mine, row_send.at[call],
                   row_recv.at[call], ((my_row + step) % rows, my_col)).start()

    def middle_sum(call):
        piece = sum_row.at[call, : rows - 1]
        pltpu.make_async_copy(piece, piece, row_recv.at[call]).wait()
        sum_col[call, my_col] = jnp.sum(sum_row[call], axis=0)
        for step in range(1, cols):
            mine = sum_col.at[call, my_col]
            remote(mine, mine, col_send.at[call],
                   col_recv.at[call], (my_row, (my_col + step) % cols)).start()

    def end_sum(call):
        piece = sum_col.at[call, : cols - 1]
        pltpu.make_async_copy(piece, piece, col_recv.at[call]).wait()
        halves_ = jnp.sum(sum_col[call], axis=0)
        return jnp.concatenate([halves_[:, :rhs], halves_[:, rhs:]], axis=0)

    spread[...] = jnp.zeros_like(spread)
    forward_own()
    boundary(0)
    backward_own(0)
    diag_copy.wait()

    def split_diag(step, carry):
        where = pl.ds(pl.multiple_of(step * span, span), span)
        high, low = split(diag_f32[where, :])
        diag_hi[where, :] = high
        diag_lo[where, :] = low
        return carry

    lax.fori_loop(0, tile // span, split_diag, 0)
    own_piece = u_f32.at[: (cols - 1) * LOW, :]
    pltpu.make_async_copy(own_piece, own_piece, own_sem.at[1]).wait()
    others = u_f32.at[: (rows - 1) * (cols - 1) * LOW, :]
    pltpu.make_async_copy(others, others, u_recv).wait()
    level = lax.broadcasted_iota(jnp.int32, (2 * LOW, tile), 0) % LOW
    empty = jnp.zeros((LOW - tail, tile), F32)

    def split_factors(step, carry):
        where = pl.ds(pl.multiple_of(step * 2 * LOW, 2 * LOW), 2 * LOW)
        first = u_f32[where, :tile]
        high, low = split(jnp.where(level < half, first, 0.0))
        u_hi[where, :] = high
        u_lo[where, :] = low
        rest = u_f32[where, tile:]
        parts = []
        for top in (0, LOW):
            parts.append(jnp.concatenate(
                [rest[top : top + tail], rest[top + tail : top + 2 * tail]], axis=1
            ))
            parts.append(empty)
        moved = pltpu.roll(first, 2 * LOW - (half - tail), 0)
        second = jnp.concatenate(parts, axis=0)
        second = jnp.where((level >= tail) & (level < half), moved, second)
        high, low = split(second)
        later = pl.ds(pl.multiple_of(total * LOW + step * 2 * LOW, 2 * LOW), 2 * LOW)
        u_hi[later, :] = high
        u_lo[later, :] = low
        return carry

    lax.fori_loop(0, total // 2, split_factors, 0)
    for c in range(len(pieces)):
        first, last, piece = returned(0, c)
        vec_z[:, first:last] = piece
        add_coeffs(c, first, last, piece)
    pl.semaphore_wait(known, rows - 1)
    send_coeffs(0)
    start_sum(gram(vec_z[...], x_ref[...]), 3)
    near = product3(dot_nn, pair[...], diag_hi[...], diag_lo[...])
    vec_n[...] = near
    own0 = gram(vec_z[...], near)
    mine = flat(coef_out, 0)
    middle_sum(3)
    turned = wait_coeffs(0)

    def far_pieces(turned):
        both = jnp.concatenate([
            jnp.concatenate([turned[:rhs], turned[rhs : 2 * rhs]], axis=1),
            jnp.concatenate([turned[2 * rhs : 3 * rhs], turned[3 * rhs :]], axis=1),
        ], axis=0)
        for c, (lo, hi) in enumerate(pieces):
            first = offset + lo if lo else 0
            last = offset + hi
            yield c, first, last, product3(
                dot_nn, both, u_hi[:, first:last], u_lo[:, first:last]
            )

    for c, first, last, piece in far_pieces(turned):
        vec_q[:, first:last] = vec_n[:, first:last] + piece
        send_halo(vec_q, 1, (c,))
    start_sum(own0 + far_gram(mine, turned), 0)
    joined[:, halo:] = stacked(vec_q[...])
    forward_own()
    rho0 = end_sum(3)
    square = (rhs, rhs)
    identity = (
        lax.broadcasted_iota(jnp.int32, square, 0) == lax.broadcasted_iota(jnp.int32, square, 1)
    ).astype(F32)
    inverse = eliminate(jnp.concatenate([rho0, identity], axis=1))[:, rhs:]
    middle_sum(0)
    boundary(1)
    backward_own(1)
    curve = end_sum(0)
    alpha0 = solved(jnp.concatenate([curve, rho0], axis=1))
    res_ref[...] = x_ref[...] - mixed(alpha0, vec_q[...])
    for c in range(len(pieces)):
        first, last, piece = returned(1, c)
        piece = vec_z[:, first:last] - mixed(alpha0, piece)
        vec_p[:, first:last] = piece
        add_coeffs(c, first, last, piece)
    send_coeffs(1)
    start_sum(gram(vec_p[...], res_ref[...]), 1)
    near = product3(dot_nn, pair[...], diag_hi[...], diag_lo[...])
    vec_n[...] = near
    own1 = gram(vec_p[...], near)
    mine = flat(coef_out, 1)
    sol_ref[...] = mixed(alpha0, vec_z[...])
    middle_sum(1)
    turned = wait_coeffs(1)
    start_sum(own1 + far_gram(mine, turned), 2)
    for c, first, last, piece in far_pieces(turned):
        vec_n[:, first:last] += piece
    middle_sum(2)
    rho1 = end_sum(1)
    beta0_t = mixed(inverse, rho1).T
    known = gram(mixed(beta0_t, curve), beta0_t)
    vec_p[...] += mixed(beta0_t, vec_z[...])
    vec_n[...] += mixed(beta0_t, vec_q[...])
    own = end_sum(2)
    alpha1 = solved(jnp.concatenate([own - known, rho1], axis=1))
    sol_ref[...] += mixed(alpha1, vec_p[...])
    res_ref[...] -= mixed(alpha1, vec_n[...])

    pltpu.make_async_copy(others, others, u_send).wait()

    @pl.when(me != total - 1)
    def _():
        for call in range(2):
            for c in range(len(pieces)):
                halo_copy(x_ref, call, c).wait_send()

    @pl.when(me != 0)
    def _():
        for call in range(2):
            for c in range(len(pieces)):
                back_copy(call, c).wait_send()

    for call in range(2):
        every = coef_out.at[call, : total - 1, :half, :]
        pltpu.make_async_copy(every, every, coef_send.at[call]).wait()
    for call in range(4):
        piece = sum_row.at[call, : rows - 1]
        pltpu.make_async_copy(piece, piece, row_send.at[call]).wait()
        piece = sum_col.at[call, : cols - 1]
        pltpu.make_async_copy(piece, piece, col_send.at[call]).wait()


def write_out(sol_ref, res_ref, sol_out, res_out, sems):
    copies = [
        pltpu.make_async_copy(sol_ref, sol_out, sems.at[0]),
        pltpu.make_async_copy(res_ref, res_out, sems.at[1]),
    ]
    for copy in copies:
        copy.start()
    for copy in copies:
        copy.wait()


def body(rows, cols, right_sides, diag_tiles, low_rank, tile_ranks, inv_factor, sub_sizes):
    rhs, tile = right_sides.shape
    spans, reach, span, _ = inv_factor.shape
    tile_rows, _, groups, _, rank, _ = low_rank.shape
    total = rows * cols
    halo = (reach - 1) * span
    lanes = tile // LANES
    factor = low_rank.reshape(tile_rows, groups, 2, rank, lanes, LANES)
    factor = factor.transpose(0, 1, 3, 4, 2, 5).reshape(-1, LANES)
    pieces, high = [], halo
    while high > 0:
        pieces.append((max(0, high - 2 * span), high))
        high = pieces[-1][0]
    count = len(pieces)
    in_hbm = pl.BlockSpec(memory_space=pltpu.HBM)
    vmem = pl.BlockSpec(memory_space=pltpu.VMEM)
    dma = pltpu.SemaphoreType.DMA
    out = jax.ShapeDtypeStruct((rhs, tile), F32)
    sizes = sub_sizes.reshape(1, -1)
    buffers = [
        pltpu.VMEM((rhs, tile), F32),
        pltpu.VMEM((spans, span, reach * span), F32),
        pltpu.VMEM((spans, 2 * span, reach * span), BF16),
        pltpu.VMEM((tile, tile), F32),
        pltpu.VMEM((tile, tile), BF16),
        pltpu.VMEM((tile, tile), BF16),
        pltpu.VMEM((total * LOW, tile + tile // 2), F32),
        pltpu.VMEM((2 * total * LOW, tile), BF16),
        pltpu.VMEM((2 * total * LOW, tile), BF16),
        pltpu.VMEM(factor.shape, F32),
        pltpu.VMEM((groups, tile_rows * LOW, tile + tile // 2), F32),
        pltpu.VMEM((2 * rhs, halo + tile), BF16),
        pltpu.VMEM((2, rhs, halo), F32),
        pltpu.VMEM((2, rhs, tile), F32),
        pltpu.VMEM((2, rhs, halo + tile), F32),
        pltpu.VMEM((spans, rhs, span), F32),
        pltpu.VMEM((spans, 2 * rhs, 2 * span), BF16),
        pltpu.VMEM((rhs, tile), F32),
        pltpu.VMEM((rhs, tile), F32),
        pltpu.VMEM((rhs, tile), F32),
        pltpu.VMEM((rhs, tile), F32),
        pltpu.VMEM((2 * rhs, tile), BF16),
        pltpu.VMEM((2 * total * LOW, 2 * rhs), F32),
        pltpu.VMEM((2 * total * LOW, rhs), F32),
        pltpu.VMEM((2, total, LOW, 2 * rhs), F32),
        pltpu.VMEM((2, total, LOW, 2 * rhs), F32),
        pltpu.VMEM((4, rows, rhs // 2, 2 * rhs), F32),
        pltpu.VMEM((4, cols, rhs // 2, 2 * rhs), F32),
        pltpu.VMEM((rhs, halo), F32),
        pltpu.VMEM(sizes.shape, jnp.int32),
    ]
    held = sum(math.prod(b.shape) * jnp.dtype(b.dtype).itemsize for b in buffers)
    grant = min(held + (8 << 20), 62 << 20)
    operands = [
        pltpu.with_memory_space_constraint(array, pltpu.HBM)
        for array in (right_sides, diag_tiles, factor, tile_ranks, inv_factor, sizes)
    ]
    results = pl.pallas_call(
        functools.partial(kernel, rows, cols, tuple(pieces), rank),
        out_shape=(pltpu.VMEM((rhs, tile), F32), pltpu.VMEM((rhs, tile), F32)),
        in_specs=[in_hbm] * 6,
        out_specs=(vmem, vmem),
        scratch_shapes=buffers + [
            pltpu.SMEM(tile_ranks.shape, jnp.int32),
            dma((spans,)), dma, dma, dma((3,)), dma((4,)), dma, dma,
            dma((2, count)), dma((2, count)), dma((2, count)), dma((2, count)),
            dma((2,)), dma((2,)), dma((4,)), dma((4,)), dma((4,)), dma((4,)),
            pltpu.SemaphoreType.REGULAR,
        ],
        compiler_params=pltpu.CompilerParams(
            collective_id=0, has_side_effects=True, vmem_limit_bytes=grant
        ),
    )(*operands)
    return pl.pallas_call(
        write_out,
        out_shape=(out, out),
        in_specs=[vmem, vmem],
        out_specs=(in_hbm, in_hbm),
        scratch_shapes=[dma((2,))],
        compiler_params=pltpu.CompilerParams(vmem_limit_bytes=1 << 20),
    )(*[pltpu.with_memory_space_constraint(result, pltpu.VMEM) for result in results])


def solution(mesh):
    rows, cols = mesh.shape["row"], mesh.shape["col"]
    placed = (
        P(None, ("row", "col")),
        P(("row", "col"), None, None),
        P("row", "col", None, None, None, None),
        P("row", "col", None),
        P(("row", "col"), None, None, None),
        P(),
    )
    return jax.shard_map(
        functools.partial(body, rows, cols),
        mesh=mesh,
        in_specs=placed,
        out_specs=(P(None, ("row", "col")), P(None, ("row", "col"))),
        check_vma=False,
    )
```

```python
import functools
import math

import jax
import jax.numpy as jnp
from jax import lax
from jax.experimental import pallas as pl
from jax.experimental.pallas import tpu as pltpu
from jax.sharding import PartitionSpec as P

MESH = pl.DeviceIdType.MESH
F32 = jnp.float32
BF16 = jnp.bfloat16
LOW = 8
LANES = 128


def split(x):
    high = x.astype(BF16)
    return high, (x - high.astype(F32)).astype(BF16)


def stacked(x):
    high, low = split(x)
    return jnp.concatenate([high, low], axis=0)


def dot_nt(a, b):
    return lax.dot_general(a, b, (((1,), (1,)), ((), ())), preferred_element_type=F32)


def dot_nn(a, b):
    return lax.dot_general(a, b, (((1,), (0,)), ((), ())), preferred_element_type=F32)


def product3(dot, both, high, low):
    rows = both.shape[0] // 2
    first = dot(both, high)
    return first[:rows] + (first[rows:] + dot(both[:rows], low))


def gram(a, b):
    return lax.dot_general(
        a, b, (((1,), (1,)), ((), ())), precision=lax.Precision.HIGHEST, preferred_element_type=F32
    )


def mixed(coeffs, rows):
    return jnp.dot(coeffs, rows, precision=lax.Precision.HIGHEST, preferred_element_type=F32)


def eliminate(work):
    count, width = work.shape
    block = 8
    row_ids = lax.broadcasted_iota(jnp.int32, work.shape, 0)
    for k in range(0, count, block):
        columns = [jnp.broadcast_to(work[:, k + j : k + j + 1], work.shape) for j in range(block)]
        rows = [work[k + i : k + i + 1, :] for i in range(block)]
        heads = [[columns[j][k + i : k + i + 1, :] for j in range(block)] for i in range(block)]
        for i in range(block):
            inverse = 1.0 / heads[i][i]
            rows[i] = rows[i] * inverse
            for j in range(i + 1, block):
                heads[i][j] = heads[i][j] * inverse
            for other in range(block):
                if other != i:
                    factor = heads[other][i]
                    rows[other] = rows[other] - factor * rows[i]
                    for j in range(i + 1, block):
                        heads[other][j] = heads[other][j] - factor * heads[i][j]
        terms = [columns[j] * rows[j] for j in range(block)]
        while len(terms) > 1:
            terms = [terms[j] + terms[j + 1] for j in range(0, len(terms), 2)]
        work = work - terms[0]
        for i in range(block):
            work = jnp.where(row_ids == k + i, rows[i], work)
    return work


def solved(work):
    return eliminate(work).T[work.shape[0] :, :]


def kernel(
    rows, cols, pieces, rank,
    x_hbm, diag_ref, factor_ref, ranks_ref, inv_ref, sizes_ref,
    sol_ref, res_ref,
    x_ref, inv_f32, inv_cat, diag_f32, diag_hi, diag_lo, u_f32, u_hi, u_lo,
    factor_f32, packed, joined, halo_in, back_in, spread, fwd, doubled, vec_z, vec_p, vec_q, vec_n, pair,
    acc_wide, acc_low, coef_out, coef_in, sum_row, sum_col, nothing, sizes_vmem, ranks,
    inv_sem, diag_sem, factor_sem, small_sem, own_sem, u_send, u_recv, halo_send, halo_recv, back_send, back_recv,
    coef_send, coef_recv, row_send, row_recv, col_send, col_recv, known,
):
    my_row, my_col = lax.axis_index("row"), lax.axis_index("col")
    total = rows * cols
    me = my_row * cols + my_col
    rhs, tile = x_hbm.shape
    spans, reach, span, _ = inv_ref.shape
    halo = (reach - 1) * span
    wide = reach * span
    offset = tile - halo
    half = rank // 2

    def coords(device):
        return (device // cols, device % cols)

    following = coords((me + 1) % total)
    previous = coords((me + total - 1) % total)

    coef_in[...] = jnp.zeros_like(coef_in)
    back_in[...] = jnp.zeros_like(back_in)
    nothing[...] = jnp.zeros_like(nothing)

    barrier = pltpu.get_barrier_semaphore()

    def greet(semaphore, device):
        pl.semaphore_signal(semaphore, inc=1, device_id=device, device_id_type=MESH)

    for turn in range(1, cols):
        greet(barrier, (my_row, (my_col + turn) % cols))
    for step in range(1, rows):
        greet(barrier, ((my_row + step) % rows, my_col))

    @pl.when((my_col == cols - 1) & (me != total - 1))
    def _():
        greet(barrier, following)

    @pl.when((my_col == 0) & (me != 0))
    def _():
        greet(barrier, previous)

    factor_copy = pltpu.make_async_copy(factor_ref, factor_f32, factor_sem)
    factor_copy.start()
    ranks_copy = pltpu.make_async_copy(ranks_ref, ranks, small_sem.at[0])
    ranks_copy.start()
    sizes_copy = pltpu.make_async_copy(sizes_ref, sizes_vmem, small_sem.at[1])
    sizes_copy.start()
    x_copy = pltpu.make_async_copy(x_hbm, x_ref, small_sem.at[2])
    x_copy.start()
    groups = rows
    tail = rank - LOW
    step_rows = 2 * (tile // LANES)

    def at_rows(ref, index, size):
        return ref.at[pl.ds(pl.multiple_of(index * size, size), size), :]

    def take(base, side, first, size, limit):
        ids = first + lax.broadcasted_iota(jnp.int32, (size, LANES), 0)
        parts = [
            factor_f32[pl.ds(base + first * step_rows + 2 * i + side, size, stride=step_rows), :]
            for i in range(tile // LANES)
        ]
        return jnp.concatenate([jnp.where(ids < limit, part, 0.0) for part in parts], axis=1)

    ranks_copy.wait()
    factor_copy.wait()
    def block(base, side, limit):
        rest = take(base, side, LOW, tail, limit)
        rest = jnp.concatenate([rest[:, : tile // 2], rest[:, tile // 2 :]], axis=0)
        return take(base, side, 0, LOW, limit), rest

    def differ(difference, most):
        square = difference * difference
        return (square + most * most - 1) // (most * most)

    def by_column(k, a):
        if rows % 4:
            return 0
        opposite = 1 - differ(k // 2 + my_row // 2 - (rows // 2 - 1), rows)
        near = 1 - differ((a - my_col) * (a - my_col) - 1, cols * cols)
        return opposite * near

    def pack(k):
        for a in range(cols):
            base = (a * groups + k) * rank * step_rows
            first, rest = block(base, 1 - by_column(k, a), ranks[a, 0, k])
            packed[k, a * LOW : (a + 1) * LOW, :tile] = first
            packed[k, a * LOW : (a + 1) * LOW, tile:] = rest
        base = (my_col * groups + k) * rank * step_rows
        where = pl.ds(pl.multiple_of((k * cols + my_col) * LOW, LOW), LOW)
        first, rest = block(base, 0, ranks[my_col, 0, k])
        u_f32[where, :tile] = first
        u_f32[where, tile:] = rest

    wraps = (1 - differ(my_col - (cols - 1), cols)) * differ(me - (total - 1), total)
    wrapped = (1 - differ(my_col, cols)) * differ(me, total)
    pl.semaphore_wait(barrier, rows + cols - 2 + wraps + wrapped)

    def remote(src, dst, send, recv, device):
        return pltpu.make_async_remote_copy(
            src_ref=src, dst_ref=dst, send_sem=send, recv_sem=recv, device_id=device,
            device_id_type=MESH,
        )

    def halo_copy(src, call, c):
        lo, hi = pieces[c]
        return remote(
            src.at[:, offset + lo : offset + hi], halo_in.at[call, :, lo:hi],
            halo_send.at[call, c], halo_recv.at[call, c], following,
        )

    def back_copy(call, c):
        lo, hi = pieces[c]
        return remote(
            spread.at[call, :, lo:hi], back_in.at[call, :, offset + lo : offset + hi],
            back_send.at[call, c], back_recv.at[call, c], previous,
        )

    def send_halo(src, call, which):
        @pl.when(me != total - 1)
        def _():
            for c in which:
                halo_copy(src, call, c).start()

        fill_first(call, which)

    def fill_first(call, which):

        @pl.when(me == 0)
        def _():
            for c in which:
                lo, hi = pieces[c]
                pltpu.make_async_copy(
                    nothing.at[:, lo:hi], halo_in.at[call, :, lo:hi], halo_recv.at[call, c]
                ).start()

    def send_back(call):
        @pl.when(me != 0)
        def _():
            for c in range(len(pieces)):
                back_copy(call, c).start()

        @pl.when(me == total - 1)
        def _():
            for c, (lo, hi) in enumerate(pieces):
                pltpu.make_async_copy(
                    nothing.at[:, lo:hi], back_in.at[call, :, offset + lo : offset + hi],
                    back_recv.at[call, c],
                ).start()

    every_piece = range(len(pieces))

    send_halo(x_hbm, 0, every_piece)

    for a in range(spans):
        for t in range(reach):
            copy = pltpu.make_async_copy(
                inv_ref.at[a, t],
                inv_f32.at[a, :, (reach - 1 - t) * span : (reach - t) * span],
                inv_sem.at[a],
            )
            copy.start()
    diag_copy = pltpu.make_async_copy(diag_ref.at[0], diag_f32, diag_sem)
    diag_copy.start()

    def send_factors(peer):
        for turn in range(1, cols):
            a = (my_col + turn) % cols
            column = by_column(peer, a)
            slot = (1 - column) * (my_row * cols + a) + column * (peer * cols + my_col)
            place = (peer + column * (my_row - peer), my_col + column * (a - my_col))
            remote(at_rows(packed.at[peer], a, LOW), at_rows(u_f32, slot, LOW),
                   u_send, u_recv, place).start()

    def pack_next(step, carry):
        pack((my_row + step) % rows)
        send_factors((my_row + step - 1) % rows)
        return carry

    pack((my_row + 1) % rows)
    lax.fori_loop(2, rows, pack_next, 0)
    pack(my_row)
    send_factors((my_row + rows - 1) % rows)
    for turn in range(1, cols):
        a = (my_col + turn) % cols
        pltpu.make_async_copy(
            at_rows(packed.at[my_row], a, LOW), at_rows(u_f32, my_row * cols + a, LOW), own_sem.at[1]
        ).start()
    for step in range(1, rows):
        greet(known, ((my_row + step) % rows, my_col))
    x_copy.wait()
    sizes_copy.wait()

    subs = sizes_ref.shape[1]
    sizes = jnp.broadcast_to(sizes_vmem[...].astype(F32), (subs, subs))
    down = lax.broadcasted_iota(jnp.int32, (subs, subs), 0)
    across = lax.broadcasted_iota(jnp.int32, (subs, subs), 1)
    opening = jnp.sum(jnp.where(across < down, sizes, 0.0), axis=1, keepdims=True)
    behind = (reach - 1) - lax.broadcasted_iota(jnp.int32, (1, wide), 1) // span
    behind = behind.astype(F32)

    joined[:, halo:] = stacked(x_ref[...])

    for a in range(spans):
        for t in range(reach):
            pltpu.make_async_copy(
                inv_ref.at[a, t], inv_f32.at[a, :, t * span : (t + 1) * span], inv_sem.at[a]
            ).wait()
        number = (me * spans + a).astype(F32)
        start = jnp.max(jnp.where(opening <= number, opening, 0.0), axis=0, keepdims=True)
        mask = jnp.where(behind <= number - start, 1.0, 0.0)
        high, low = split(inv_f32[a] * mask)
        inv_cat[a, :span] = high
        inv_cat[a, span:] = low


    def quarters(product):
        first = product[:rhs, :span]
        return first + (product[rhs:, :span] + (product[:rhs, span:] + product[rhs:, span:]))

    def halves(product):
        return product[:rhs] + product[rhs:]

    def forward_own():
        for a in range(spans):
            skip = max(0, halo - a * span)
            fwd[a] = quarters(
                dot_nt(joined[:, a * span + skip : a * span + wide], inv_cat[a, :, skip:])
            )

    def finish(a):
        both = stacked(fwd[a])
        doubled[a] = jnp.concatenate([both, both], axis=1)

    def boundary(call):
        for a in range(spans):
            if a * span >= halo:
                finish(a)
        for c, (lo, hi) in enumerate(pieces):
            halo_copy(x_ref, call, c).wait_recv()
            joined[:, lo:hi] = stacked(halo_in[call, :, lo:hi])
            for a in range(spans):
                first = max(lo, a * span)
                if first < hi:
                    fwd[a] += quarters(dot_nt(
                        joined[:, first:hi], inv_cat[a, :, first - a * span : hi - a * span]
                    ))
            for a in range(spans):
                if lo <= a * span < hi:
                    finish(a)
                    spread[call, :, a * span : halo] += halves(
                        dot_nn(doubled[a], inv_cat[a, :, : halo - a * span])
                    )
        send_back(call)

    def backward_own(call):
        for a in range(spans):
            skip = max(0, halo - a * span)
            spread[call, :, a * span + skip : a * span + wide] += halves(
                dot_nn(doubled[a], inv_cat[a, :, skip:])
            )

    def returned(call, c):
        lo, hi = pieces[c]
        back_copy(call, c).wait_recv()
        first = offset + lo if lo else 0
        last = offset + hi
        return first, last, spread[call, :, halo + first : halo + last] + back_in[call, :, first:last]

    def add_coeffs(c, first, last, piece):
        both = stacked(piece)
        pair[:, first:last] = both
        wide_part = dot_nt(u_hi[:, first:last], both)
        low_part = dot_nt(u_lo[:, first:last], both[:rhs])
        if c:
            acc_wide[...] += wide_part
            acc_low[...] += low_part
        else:
            acc_wide[...] = wide_part
            acc_low[...] = low_part

    def send_coeffs(call):
        coeffs = acc_wide[:, :rhs] + (acc_wide[:, rhs:] + acc_low[...])
        middle = total * LOW
        coef_out[call, :, :, :rhs] = coeffs[:middle].reshape(total, LOW, rhs)
        coef_out[call, :, :, rhs:] = coeffs[middle:].reshape(total, LOW, rhs)

        def send(peer_row, peer_col):
            remote(coef_out.at[call, peer_row * cols + peer_col, :half, :],
                   coef_in.at[call, me, :half, :],
                   coef_send.at[call], coef_recv.at[call], (peer_row, peer_col)).start()

        low_side = 1 - my_col // (cols // 2)

        for n in range(cols - 1):
            far = low_side * (cols - 1 - n) + (1 - low_side) * n
            beyond = (far - my_col + cols - 1) // cols
            before = (my_col - far + cols - 1) // cols
            far = far - low_side * (1 - beyond) + (1 - low_side) * (1 - before)
            for step in range(rows):
                send((my_row + step) % rows, far)
        for step in range(1, rows):
            send((my_row + step) % rows, my_col)
        pltpu.make_async_copy(
            coef_out.at[call, me], coef_in.at[call, me], own_sem.at[2 + call]
        ).start()

    def flat(ref, call):
        return stacked(ref[call].reshape(total * LOW, 2 * rhs).T)

    def sided(ref, call):
        return jnp.concatenate(split(ref[call].reshape(total * LOW, 2 * rhs)), axis=1)

    def wait_coeffs(call):
        every = coef_out.at[call, : total - 1, :half, :]
        pltpu.make_async_copy(every, every, coef_recv.at[call]).wait()
        pltpu.make_async_copy(
            coef_out.at[call, me], coef_in.at[call, me], own_sem.at[2 + call]
        ).wait()

    def far_gram(mine, call):
        product = dot_nn(mine, sided(coef_in, call))
        width = 2 * rhs
        square = product[:width, :width] + (
            product[width:, :width] + (product[:width, width:] + product[width:, width:])
        )
        return square[:rhs, :rhs] + square[rhs:, rhs:]

    height = rhs // 2

    def start_sum(value, call):
        sum_row[call, my_row] = jnp.concatenate([value[:height], value[height:]], axis=1)
        for step in range(1, rows):
            mine = sum_row.at[call, my_row]
            remote(mine, mine, row_send.at[call],
                   row_recv.at[call], ((my_row + step) % rows, my_col)).start()

    def middle_sum(call):
        piece = sum_row.at[call, : rows - 1]
        pltpu.make_async_copy(piece, piece, row_recv.at[call]).wait()
        sum_col[call, my_col] = jnp.sum(sum_row[call], axis=0)
        for step in range(1, cols):
            mine = sum_col.at[call, my_col]
            remote(mine, mine, col_send.at[call],
                   col_recv.at[call], (my_row, (my_col + step) % cols)).start()

    def end_sum(call):
        piece = sum_col.at[call, : cols - 1]
        pltpu.make_async_copy(piece, piece, col_recv.at[call]).wait()
        halves_ = jnp.sum(sum_col[call], axis=0)
        return jnp.concatenate([halves_[:, :rhs], halves_[:, rhs:]], axis=0)

    spread[...] = jnp.zeros_like(spread)
    forward_own()
    boundary(0)
    backward_own(0)
    diag_copy.wait()

    def split_diag(step, carry):
        where = pl.ds(pl.multiple_of(step * span, span), span)
        high, low = split(diag_f32[where, :])
        diag_hi[where, :] = high
        diag_lo[where, :] = low
        return carry

    lax.fori_loop(0, tile // span, split_diag, 0)
    own_piece = u_f32.at[: (cols - 1) * LOW, :]
    pltpu.make_async_copy(own_piece, own_piece, own_sem.at[1]).wait()
    others = u_f32.at[: (rows - 1) * (cols - 1) * LOW, :]
    pltpu.make_async_copy(others, others, u_recv).wait()
    level = lax.broadcasted_iota(jnp.int32, (2 * LOW, tile), 0) % LOW
    empty = jnp.zeros((LOW - tail, tile), F32)

    def split_factors(step, carry):
        where = pl.ds(pl.multiple_of(step * 2 * LOW, 2 * LOW), 2 * LOW)
        first = u_f32[where, :tile]
        high, low = split(jnp.where(level < half, first, 0.0))
        u_hi[where, :] = high
        u_lo[where, :] = low
        rest = u_f32[where, tile:]
        parts = []
        for top in (0, LOW):
            parts.append(jnp.concatenate(
                [rest[top : top + tail], rest[top + tail : top + 2 * tail]], axis=1
            ))
            parts.append(empty)
        moved = pltpu.roll(first, 2 * LOW - (half - tail), 0)
        second = jnp.concatenate(parts, axis=0)
        second = jnp.where((level >= tail) & (level < half), moved, second)
        high, low = split(second)
        later = pl.ds(pl.multiple_of(total * LOW + step * 2 * LOW, 2 * LOW), 2 * LOW)
        u_hi[later, :] = high
        u_lo[later, :] = low
        return carry

    lax.fori_loop(0, total // 2, split_factors, 0)
    for c in range(len(pieces)):
        first, last, piece = returned(0, c)
        vec_z[:, first:last] = piece
        add_coeffs(c, first, last, piece)
    pl.semaphore_wait(known, rows - 1)
    send_coeffs(0)
    start_sum(gram(vec_z[...], x_ref[...]), 3)
    near = product3(dot_nn, pair[...], diag_hi[...], diag_lo[...])
    vec_n[...] = near
    own0 = gram(vec_z[...], near)
    mine = flat(coef_out, 0)
    middle_sum(3)
    wait_coeffs(0)

    def far_pieces(call):
        turned = flat(coef_in, call)
        both = jnp.concatenate([
            jnp.concatenate([turned[:rhs], turned[rhs : 2 * rhs]], axis=1),
            jnp.concatenate([turned[2 * rhs : 3 * rhs], turned[3 * rhs :]], axis=1),
        ], axis=0)
        for c, (lo, hi) in enumerate(pieces):
            first = offset + lo if lo else 0
            last = offset + hi
            yield c, first, last, product3(
                dot_nn, both, u_hi[:, first:last], u_lo[:, first:last]
            )

    for c, first, last, piece in far_pieces(0):
        vec_q[:, first:last] = vec_n[:, first:last] + piece
        send_halo(vec_q, 1, (c,))
    start_sum(own0 + far_gram(mine, 0), 0)
    joined[:, halo:] = stacked(vec_q[...])
    forward_own()
    rho0 = end_sum(3)
    square = (rhs, rhs)
    identity = (
        lax.broadcasted_iota(jnp.int32, square, 0) == lax.broadcasted_iota(jnp.int32, square, 1)
    ).astype(F32)
    inverse = eliminate(jnp.concatenate([rho0, identity], axis=1))[:, rhs:]
    middle_sum(0)
    boundary(1)
    backward_own(1)
    curve = end_sum(0)
    alpha0 = solved(jnp.concatenate([curve, rho0], axis=1))
    res_ref[...] = x_ref[...] - mixed(alpha0, vec_q[...])
    for c in range(len(pieces)):
        first, last, piece = returned(1, c)
        piece = vec_z[:, first:last] - mixed(alpha0, piece)
        vec_p[:, first:last] = piece
        add_coeffs(c, first, last, piece)
    send_coeffs(1)
    start_sum(gram(vec_p[...], res_ref[...]), 1)
    near = product3(dot_nn, pair[...], diag_hi[...], diag_lo[...])
    vec_n[...] = near
    own1 = gram(vec_p[...], near)
    mine = flat(coef_out, 1)
    sol_ref[...] = mixed(alpha0, vec_z[...])
    middle_sum(1)
    wait_coeffs(1)
    start_sum(own1 + far_gram(mine, 1), 2)
    for c, first, last, piece in far_pieces(1):
        vec_n[:, first:last] += piece
    middle_sum(2)
    rho1 = end_sum(1)
    beta0_t = mixed(inverse, rho1).T
    known = gram(mixed(beta0_t, curve), beta0_t)
    vec_p[...] += mixed(beta0_t, vec_z[...])
    vec_n[...] += mixed(beta0_t, vec_q[...])
    own = end_sum(2)
    alpha1 = solved(jnp.concatenate([own - known, rho1], axis=1))
    sol_ref[...] += mixed(alpha1, vec_p[...])
    res_ref[...] -= mixed(alpha1, vec_n[...])

    pltpu.make_async_copy(others, others, u_send).wait()

    @pl.when(me != total - 1)
    def _():
        for call in range(2):
            for c in range(len(pieces)):
                halo_copy(x_ref, call, c).wait_send()

    @pl.when(me != 0)
    def _():
        for call in range(2):
            for c in range(len(pieces)):
                back_copy(call, c).wait_send()

    for call in range(2):
        every = coef_out.at[call, : total - 1, :half, :]
        pltpu.make_async_copy(every, every, coef_send.at[call]).wait()
    for call in range(4):
        piece = sum_row.at[call, : rows - 1]
        pltpu.make_async_copy(piece, piece, row_send.at[call]).wait()
        piece = sum_col.at[call, : cols - 1]
        pltpu.make_async_copy(piece, piece, col_send.at[call]).wait()


def write_out(sol_ref, res_ref, sol_out, res_out, sems):
    copies = [
        pltpu.make_async_copy(sol_ref, sol_out, sems.at[0]),
        pltpu.make_async_copy(res_ref, res_out, sems.at[1]),
    ]
    for copy in copies:
        copy.start()
    for copy in copies:
        copy.wait()


def body(rows, cols, right_sides, diag_tiles, low_rank, tile_ranks, inv_factor, sub_sizes):
    rhs, tile = right_sides.shape
    spans, reach, span, _ = inv_factor.shape
    tile_rows, _, groups, _, rank, _ = low_rank.shape
    total = rows * cols
    halo = (reach - 1) * span
    lanes = tile // LANES
    factor = low_rank.reshape(tile_rows, groups, 2, rank, lanes, LANES)
    factor = factor.transpose(0, 1, 3, 4, 2, 5).reshape(-1, LANES)
    pieces, high = [], halo
    while high > 0:
        pieces.append((max(0, high - 2 * span), high))
        high = pieces[-1][0]
    count = len(pieces)
    in_hbm = pl.BlockSpec(memory_space=pltpu.HBM)
    vmem = pl.BlockSpec(memory_space=pltpu.VMEM)
    dma = pltpu.SemaphoreType.DMA
    out = jax.ShapeDtypeStruct((rhs, tile), F32)
    sizes = sub_sizes.reshape(1, -1)
    buffers = [
        pltpu.VMEM((rhs, tile), F32),
        pltpu.VMEM((spans, span, reach * span), F32),
        pltpu.VMEM((spans, 2 * span, reach * span), BF16),
        pltpu.VMEM((tile, tile), F32),
        pltpu.VMEM((tile, tile), BF16),
        pltpu.VMEM((tile, tile), BF16),
        pltpu.VMEM((total * LOW, tile + tile // 2), F32),
        pltpu.VMEM((2 * total * LOW, tile), BF16),
        pltpu.VMEM((2 * total * LOW, tile), BF16),
        pltpu.VMEM(factor.shape, F32),
        pltpu.VMEM((groups, tile_rows * LOW, tile + tile // 2), F32),
        pltpu.VMEM((2 * rhs, halo + tile), BF16),
        pltpu.VMEM((2, rhs, halo), F32),
        pltpu.VMEM((2, rhs, tile), F32),
        pltpu.VMEM((2, rhs, halo + tile), F32),
        pltpu.VMEM((spans, rhs, span), F32),
        pltpu.VMEM((spans, 2 * rhs, 2 * span), BF16),
        pltpu.VMEM((rhs, tile), F32),
        pltpu.VMEM((rhs, tile), F32),
        pltpu.VMEM((rhs, tile), F32),
        pltpu.VMEM((rhs, tile), F32),
        pltpu.VMEM((2 * rhs, tile), BF16),
        pltpu.VMEM((2 * total * LOW, 2 * rhs), F32),
        pltpu.VMEM((2 * total * LOW, rhs), F32),
        pltpu.VMEM((2, total, LOW, 2 * rhs), F32),
        pltpu.VMEM((2, total, LOW, 2 * rhs), F32),
        pltpu.VMEM((4, rows, rhs // 2, 2 * rhs), F32),
        pltpu.VMEM((4, cols, rhs // 2, 2 * rhs), F32),
        pltpu.VMEM((rhs, halo), F32),
        pltpu.VMEM(sizes.shape, jnp.int32),
    ]
    held = sum(math.prod(b.shape) * jnp.dtype(b.dtype).itemsize for b in buffers)
    grant = min(held + (8 << 20), 62 << 20)
    operands = [
        pltpu.with_memory_space_constraint(array, pltpu.HBM)
        for array in (right_sides, diag_tiles, factor, tile_ranks, inv_factor, sizes)
    ]
    results = pl.pallas_call(
        functools.partial(kernel, rows, cols, tuple(pieces), rank),
        out_shape=(pltpu.VMEM((rhs, tile), F32), pltpu.VMEM((rhs, tile), F32)),
        in_specs=[in_hbm] * 6,
        out_specs=(vmem, vmem),
        scratch_shapes=buffers + [
            pltpu.SMEM(tile_ranks.shape, jnp.int32),
            dma((spans,)), dma, dma, dma((3,)), dma((4,)), dma, dma,
            dma((2, count)), dma((2, count)), dma((2, count)), dma((2, count)),
            dma((2,)), dma((2,)), dma((4,)), dma((4,)), dma((4,)), dma((4,)),
            pltpu.SemaphoreType.REGULAR,
        ],
        compiler_params=pltpu.CompilerParams(
            collective_id=0, has_side_effects=True, vmem_limit_bytes=grant
        ),
    )(*operands)
    return pl.pallas_call(
        write_out,
        out_shape=(out, out),
        in_specs=[vmem, vmem],
        out_specs=(in_hbm, in_hbm),
        scratch_shapes=[dma((2,))],
        compiler_params=pltpu.CompilerParams(vmem_limit_bytes=1 << 20),
    )(*[pltpu.with_memory_space_constraint(result, pltpu.VMEM) for result in results])


def solution(mesh):
    rows, cols = mesh.shape["row"], mesh.shape["col"]
    placed = (
        P(None, ("row", "col")),
        P(("row", "col"), None, None),
        P("row", "col", None, None, None, None),
        P("row", "col", None),
        P(("row", "col"), None, None, None),
        P(),
    )
    return jax.shard_map(
        functools.partial(body, rows, cols),
        mesh=mesh,
        in_specs=placed,
        out_specs=(P(None, ("row", "col")), P(None, ("row", "col"))),
        check_vma=False,
    )
```
